32 devices in a mesh: grp: 2 (over y), seq: 16 (over z, x, core).
Axes of the slice: x: 2, y: 2, z: 4, core: 2. Of those that a mesh axis runs over, the one named last changes fastest.
Arguments:
- inputs: bfloat16 [4, 2048, 1536], P('grp', 'seq'), parts along dimension 0, may hold values from -36 to 36
- gain: float32 [1536], replicated, may hold values from 0.1 to 1.9
- conv_weight: bfloat16 [3, 1536, 768], P(None, 'seq'), may hold values from -0.09375 to 0.09375
- proj_weight: bfloat16 [768, 1536], P(None, 'seq'), may hold values from -0.21875 to 0.21875
- head_weight: bfloat16 [1536, 512], P(None, 'seq'), may hold values from -0.15625 to 0.15625
- track_head_bias: bfloat16 [1, 512], P(None, 'seq'), may hold values from -4 to 4
- counts: int32 [4, 2048, 512], P('grp', 'seq'), parts along dimension 0, may hold values from 0 to 32
Outputs:
- input_grad: bfloat16 [4, 2048, 1536], P('grp', 'seq'), parts along dimension 0
- loss_value: float32 [2], P('grp'), parts along dimension 0
The draws below stay inside these ranges and needn't reach their ends.
There are 2 independent parts, one for each index of `grp`. The reference program is written for one: setup_inputs(seed, part) draws one part's arguments, and reference() takes and returns one part's arrays. A program takes and returns all parts, laid end to end along the dimension named above; an argument that names none is the same for every part. Nothing has to cross between parts.
All inputs are finite; a program needn't handle non-finite values.
Results may differ from the reference program's by a relative error of at most 0.011.
Values may be sent and summed in bfloat16 or wider, within the bound.
A program may use at most 128 MiB of HBM per device.

```python
import math
import jax
import jax.numpy as jnp
from jax import lax

C = 1536
H = 768
GROUP_SEQUENCES = 2
SEQUENCE_BINS = 2048
TRACKS = 512
DILATION_BINS = 1024


def draw_inputs(key, part):
    key_rows = jax.random.fold_in(key, 11)
    key_cols = jax.random.fold_in(key, 12)
    key_base = jax.random.fold_in(key, 13)
    row_scale = jnp.exp(jax.random.uniform(key_rows, (GROUP_SEQUENCES, SEQUENCE_BINS, 1), jnp.float32, math.log(0.3), math.log(3.0)))
    col_scale = jnp.exp(jax.random.uniform(key_cols, (1, 1, C), jnp.float32, math.log(0.3), math.log(3.0)))
    base = jax.random.normal(key_base, (GROUP_SEQUENCES, SEQUENCE_BINS, C), jnp.float32)
    base = jnp.clip(base, -4.0, 4.0)
    return (base * row_scale * col_scale).astype(jnp.bfloat16)


def draw_counts(key, part):
    positions = jnp.arange(SEQUENCE_BINS, dtype=jnp.int32).reshape(1, SEQUENCE_BINS, 1)
    levels = 2 + 30 * positions // max(SEQUENCE_BINS - 1, 1)
    return jax.random.randint(jax.random.fold_in(key, 21), (GROUP_SEQUENCES, SEQUENCE_BINS, TRACKS), 0, levels + 1, dtype=jnp.int32)


def block_scale(stream_key, shape, pieces, low, high):
    def one(dim, shards_of):
        draws = jax.random.uniform(jax.random.fold_in(jax.random.fold_in(stream_key, 6), dim), (shards_of,), jnp.float32, low / len(pieces), high / len(pieces))
        return jnp.repeat(jnp.exp(draws), shape[dim] // shards_of).reshape((-1,) + (1,) * (len(shape) - dim - 1))

    loudness = one(*pieces[0])
    for cut in pieces[1:]:
        loudness = loudness * one(*cut)
    return loudness


def noise(rng, dims, width, reach, split=(), held_as=jnp.bfloat16):
    values = jax.random.normal(rng, dims, jnp.float32) * width
    if len(split) > 0:
        values = block_scale(rng, dims, split, -0.22, 0.18) * values
    return jnp.clip(values, min=-reach, max=reach).astype(held_as)


def setup_inputs(seed: int = 0, part: int = 0) -> dict:
    splits = jax.random.split(jax.random.key(seed), 8)
    own_keys = jax.random.split(jax.random.fold_in(splits[7], part), 8)
    return {
        "inputs": draw_inputs(jax.random.fold_in(jax.random.fold_in(splits[7], part), 71), part),
        "gain": jnp.clip(1.0 + 0.18 * jax.random.normal(splits[1], (C,), jnp.float32), 0.1, 1.9),
        "conv_weight": noise(splits[2], (3, C, H), (3 * C) ** -0.5, 0.09375, ((1, 16),)),
        "proj_weight": noise(splits[3], (H, C), H ** -0.5, 0.21875, ((1, 16),)),
        "head_weight": noise(splits[4], (C, TRACKS), C ** -0.5, 0.15625, ((1, 16),)),
        "track_head_bias": noise(splits[5], (1, TRACKS), 1.0, 4.0, ((1, 16),)),
        "counts": draw_counts(jax.random.fold_in(jax.random.fold_in(splits[7], part), 71), part),
    }


def norm_rows(value_entries, gain):
    scale_inv = lax.rsqrt(lax.optimization_barrier(jnp.mean(value_entries * value_entries, axis=-1, keepdims=True)) + 1e-06)
    return value_entries * scale_inv * gain

def head_block(stream, head_full, bias_full, observed):
    logits = jnp.dot(stream, head_full, preferred_element_type=jnp.float32) + bias_full.astype(jnp.float32)
    poisson_rate = jax.nn.softplus(logits) + 0.05
    observed_f = observed.astype(jnp.float32)
    loss_total = jnp.sum(poisson_rate - observed_f * jnp.log(poisson_rate))
    logit_grad = ((1.0 - observed_f / poisson_rate) * jax.nn.sigmoid(logits)).astype(jnp.bfloat16)
    residual_gradient = lax.dot_general(logit_grad, head_full, (((1,), (1,)), ((), ())), preferred_element_type=jnp.float32)
    return (loss_total, residual_gradient)

def back_dot(left, right):
    return lax.dot_general(left, right, (((1,), (1,)), ((), ())), preferred_element_type=jnp.float32)

def move_back(value_entries, window_width):
    zeroed_rows = jnp.zeros((GROUP_SEQUENCES, DILATION_BINS, window_width), value_entries.dtype)
    return jnp.concatenate([zeroed_rows, value_entries[:, :SEQUENCE_BINS - DILATION_BINS]], axis=1)

def move_ahead(value_entries, window_width):
    zeroed_rows = jnp.zeros((GROUP_SEQUENCES, DILATION_BINS, window_width), value_entries.dtype)
    return jnp.concatenate([value_entries[:, DILATION_BINS:], zeroed_rows], axis=1)

def reference(inputs, gain, conv_weight, proj_weight, head_weight, track_head_bias, counts):
    rows_all = GROUP_SEQUENCES * SEQUENCE_BINS
    inputs_f = inputs.astype(jnp.float32)
    normed = norm_rows(inputs_f, gain).astype(jnp.bfloat16)
    behind_rows = move_back(normed, C).reshape(rows_all, C)
    ahead_rows = move_ahead(normed, C).reshape(rows_all, C)
    conv_pre = jnp.dot(behind_rows, conv_weight[0], preferred_element_type=jnp.float32)
    conv_pre = conv_pre + jnp.dot(normed.reshape(rows_all, C), conv_weight[1], preferred_element_type=jnp.float32)
    conv_pre = conv_pre + jnp.dot(ahead_rows, conv_weight[2], preferred_element_type=jnp.float32)
    conv_act = jax.nn.gelu(conv_pre).astype(jnp.bfloat16)
    stream = (inputs_f.reshape(rows_all, C) + jnp.dot(conv_act, proj_weight, preferred_element_type=jnp.float32)).astype(jnp.bfloat16)
    block_rows = math.gcd(SEQUENCE_BINS, 1024)

    def per_block(paired):
        return head_block(paired[0], head_weight, track_head_bias, paired[1])
    totals, residual_gradient = lax.map(per_block, (stream.reshape(-1, block_rows, C), counts.reshape(-1, block_rows, TRACKS)))
    residual_gradient = residual_gradient.reshape(rows_all, C)
    loss_value = (jnp.sum(totals) / (GROUP_SEQUENCES * SEQUENCE_BINS * TRACKS)).reshape(1)
    act_grad = back_dot(residual_gradient.astype(jnp.bfloat16), proj_weight)
    _, gelu_back = jax.vjp(jax.nn.gelu, conv_pre)
    pre_grad = gelu_back(act_grad)[0].astype(jnp.bfloat16)
    pre_three = pre_grad.reshape(GROUP_SEQUENCES, SEQUENCE_BINS, H)
    grad_ahead = move_ahead(pre_three, H).reshape(rows_all, H)
    grad_behind = move_back(pre_three, H).reshape(rows_all, H)
    normed_grad = back_dot(grad_ahead, conv_weight[0]) + back_dot(pre_grad, conv_weight[1]) + back_dot(grad_behind, conv_weight[2])
    _, norm_back = jax.vjp(lambda value_entries: norm_rows(value_entries, gain), inputs_f)
    input_grad = (residual_gradient.reshape(GROUP_SEQUENCES, SEQUENCE_BINS, C) + norm_back(normed_grad.reshape(GROUP_SEQUENCES, SEQUENCE_BINS, C))[0]).astype(jnp.bfloat16)
    return (input_grad, loss_value)
```

```python
import functools

import jax
import jax.experimental.pallas as pl
import jax.experimental.pallas.tpu as pltpu
import jax.numpy as jnp
from jax import lax
from jax.sharding import PartitionSpec as P

SPAN = 8
MESH = pl.DeviceIdType.MESH
LANES = 128
EPS = 1e-06
GELU_K = 0.7978845608028654
GELU_C = 0.044715


def shifted(value, axis, steps):
    count = lax.axis_size(axis)
    initial, last = (max(0, -steps), min(count, count - steps))
    return lax.ppermute(value, axis, [(source, source + steps) for source in range(initial, last)])


def norm_rows(value_entries, gain):
    scale_inv = lax.rsqrt(jnp.mean(value_entries * value_entries, axis=-1, keepdims=True) + 1e-06)
    return value_entries * scale_inv * gain


def head_block(stream, head_full, bias_full, observed):
    logits = jnp.dot(stream, head_full, preferred_element_type=jnp.float32) + bias_full.astype(
        jnp.float32
    )
    poisson_rate = jax.nn.softplus(logits) + 0.05
    observed_f = observed.astype(jnp.float32)
    loss_total = jnp.sum(poisson_rate - observed_f * jnp.log(poisson_rate))
    logit_grad = ((1.0 - observed_f / poisson_rate) * jax.nn.sigmoid(logits)).astype(jnp.bfloat16)
    residual_gradient = lax.dot_general(
        logit_grad, head_full, (((1,), (1,)), ((), ())), preferred_element_type=jnp.float32
    )
    return (loss_total, residual_gradient)


def back_dot(left, right):
    return lax.dot_general(
        left, right, (((1,), (1,)), ((), ())), preferred_element_type=jnp.float32
    )


def shards(inputs, gain, conv_weight, proj_weight, head_weight, track_head_bias, counts):
    seq_count, row_count, window_width = inputs.shape
    flat_rows = seq_count * row_count
    track_count = counts.shape[2]
    conv_full, proj_full = (
        lax.all_gather(conv_weight, "seq", axis=1, tiled=True),
        lax.all_gather(proj_weight, "seq", axis=1, tiled=True),
    )
    inner = conv_full.shape[2]
    inputs_f = inputs.astype(jnp.float32)
    normed = norm_rows(inputs_f, gain).astype(jnp.bfloat16)
    normed_flat = normed.reshape(flat_rows, window_width)
    behind_rows = shifted(normed, "seq", SPAN).reshape(flat_rows, window_width)
    ahead_rows = shifted(normed, "seq", -SPAN).reshape(flat_rows, window_width)
    conv_pre = jnp.dot(normed_flat, conv_full[1], preferred_element_type=jnp.float32)
    conv_pre = conv_pre + jnp.dot(behind_rows, conv_full[0], preferred_element_type=jnp.float32)
    conv_pre = conv_pre + jnp.dot(ahead_rows, conv_full[2], preferred_element_type=jnp.float32)
    conv_act = jax.nn.gelu(conv_pre).astype(jnp.bfloat16)
    stream = (
        inputs_f.reshape(flat_rows, window_width)
        + jnp.dot(conv_act, proj_full, preferred_element_type=jnp.float32)
    ).astype(jnp.bfloat16)
    counts_flat = counts.reshape(flat_rows, track_count)
    head_full, bias_full = (
        lax.all_gather(head_weight, "seq", axis=1, tiled=True),
        lax.all_gather(track_head_bias, "seq", axis=1, tiled=True),
    )
    loss_total, residual_gradient = head_block(stream, head_full, bias_full, counts_flat)
    summed_loss = lax.psum(loss_total, "seq")
    loss_value = (summed_loss / (flat_rows * lax.axis_size("seq") * track_count)).reshape(1)
    act_grad = back_dot(residual_gradient.astype(jnp.bfloat16), proj_full)
    _, gelu_back = jax.vjp(jax.nn.gelu, conv_pre)
    pre_grad = gelu_back(act_grad)[0].astype(jnp.bfloat16)
    pre_three = pre_grad.reshape(seq_count, row_count, inner)
    grad_ahead = shifted(pre_three, "seq", -SPAN).reshape(flat_rows, inner)
    grad_behind = shifted(pre_three, "seq", SPAN).reshape(flat_rows, inner)
    normed_grad = back_dot(pre_grad, conv_full[1])
    normed_grad = normed_grad + back_dot(grad_ahead, conv_full[0])
    normed_grad = normed_grad + back_dot(grad_behind, conv_full[2])
    _, norm_back = jax.vjp(lambda value_entries: norm_rows(value_entries, gain), inputs_f)
    input_grad = (
        residual_gradient.reshape(seq_count, row_count, window_width)
        + norm_back(normed_grad.reshape(seq_count, row_count, window_width))[0]
    ).astype(jnp.bfloat16)
    return (input_grad, loss_value)


def dot_nn(left, right):
    return jnp.dot(left, right, preferred_element_type=jnp.float32)


def block_kernel(
    n, bins_total, x_ref, gain_ref, conv_ref, proj_ref, head_ref, counts_ref, out_ref, loss_ref,
    convf, projf, headf, normed, q_out, q_in, pre, act, stream, res, pg, pg_in, ng, losses,
    z_send, z_recv, x_send, x_recv, c_send, c_recv, q_send, q_recv, g_send, g_recv, l_send, l_recv,
):
    me = lax.axis_index("seq")
    nz = n // 4
    core = me % 2
    col = (me // 2) % 2
    z = me // 4
    low = z // (nz // 2)
    tap = 2 * low
    partner = (me + n // 2) % n
    x_peer = z * 4 + (1 - col) * 2 + core
    c_peer = z * 4 + col * 2 + (1 - core)
    rows, width = x_ref.shape
    inner = convf.shape[2]
    depths = (conv_ref.shape[1], proj_ref.shape[0], head_ref.shape[0])
    shards_in = (conv_ref, proj_ref, head_ref)
    fulls = (convf, projf, headf)

    def place(u, zs, xs, cs, part):
        depth = depths[u]
        start = pl.multiple_of((zs * 4 + xs * 2 + cs) * depth, depth)
        if u == 0:
            taps = pl.ds(low, 2) if part else slice(None)
            return convf.at[taps, pl.ds(start, depth), :]
        return fulls[u].at[pl.ds(start, depth), :]

    def mine(u, part):
        if u == 0 and part:
            return conv_ref.at[pl.ds(low, 2)]
        return shards_in[u]

    def remote(src, dst, send, recv, target):
        return pltpu.make_async_remote_copy(
            src_ref=src, dst_ref=dst, send_sem=send, recv_sem=recv,
            device_id={"seq": target}, device_id_type=MESH,
        )

    def z_copy(u, zs, way, own=False):
        dst = place(u, zs, col, core, False)
        src = mine(u, False) if own else dst
        return remote(src, dst, z_send.at[u, zs, way], z_recv.at[u, zs], me + (4 if way == 0 else -4))

    def x_copy(u, zs, own=False):
        dst = place(u, zs, col, core, True)
        src = mine(u, True) if own else dst
        return remote(src, dst, x_send.at[u, zs], x_recv.at[u, zs], x_peer)

    def c_copy(u, zs, xs, own=False):
        dst = place(u, zs, xs, core, True)
        src = mine(u, True) if own else dst
        return remote(src, dst, c_send.at[u, zs, xs], c_recv.at[u, zs, xs], c_peer)

    def own_sends(u):
        @pl.when(z < nz - 1)
        def _():
            z_copy(u, z, 0, True).start()

        @pl.when(z > 0)
        def _():
            z_copy(u, z, 1, True).start()

        x_copy(u, z, True).start()
        c_copy(u, z, col, True).start()

    def z_events(u):
        for step in range(1, nz):
            @pl.when(z - step >= 0)
            def _():
                zs = z - step
                z_copy(u, zs, 0).wait_recv()

                @pl.when(z < nz - 1)
                def _():
                    z_copy(u, zs, 0).start()

                x_copy(u, zs).start()
                c_copy(u, zs, col).start()

            @pl.when(z + step < nz)
            def _():
                zs = z + step
                z_copy(u, zs, 1).wait_recv()

                @pl.when(z > 0)
                def _():
                    z_copy(u, zs, 1).start()

                x_copy(u, zs).start()
                c_copy(u, zs, col).start()

    def arrived(u, zs, xs, cs, sem):
        dst = place(u, zs, xs, cs, True)
        return remote(dst, dst, sem, sem, me)

    def x_events(u):
        for step in range(nz):
            zs = (z + step) % nz
            pltpu.make_async_remote_copy(
                src_ref=place(u, zs, 1 - col, core, True), dst_ref=place(u, zs, 1 - col, core, True),
                send_sem=x_send.at[u, zs], recv_sem=x_recv.at[u, zs],
                device_id={"seq": x_peer}, device_id_type=MESH,
            ).wait_recv()
            c_copy(u, zs, 1 - col).start()

    def c_waits(u):
        for xs in range(2):
            for zs in range(nz):
                dst = place(u, zs, xs, 1 - core, True)
                remote(dst, dst, c_send.at[u, zs, xs], c_recv.at[u, zs, xs], c_peer).wait_recv()

    barrier = pltpu.get_barrier_semaphore()
    for off in range(1, n):
        pl.semaphore_signal(barrier, inc=1, device_id={"seq": (me + off) % n}, device_id_type=MESH)
    pl.semaphore_wait(barrier, n - 1)

    own_sends(0)
    for u in range(3):
        depth = depths[u]
        start = pl.multiple_of(me * depth, depth)
        if u == 0:
            convf[:, pl.ds(start, depth), :] = conv_ref[...]
        else:
            fulls[u][pl.ds(start, depth), :] = shards_in[u][...]
    xf = x_ref[...].astype(jnp.float32)
    scale = lax.rsqrt(jnp.mean(xf * xf, axis=-1, keepdims=True) + EPS)
    normed[...] = (xf * scale * gain_ref[...]).astype(jnp.bfloat16)
    z_events(0)
    own_sends(1)
    own_sends(2)
    x_events(0)
    c_waits(0)

    chunks = q_out.shape[0]
    wide = inner // chunks

    def q_copy(k):
        return remote(q_out.at[k], q_in.at[k], q_send.at[k], q_recv.at[k], partner)

    def g_copy(k):
        return remote(pg.at[k], pg_in.at[k], g_send.at[k], g_recv.at[k], partner)

    for k in range(chunks):
        cols = slice(k * wide, (k + 1) * wide)
        q_out[k] = dot_nn(normed[...], convf[tap, :, cols]).astype(jnp.bfloat16)
        q_copy(k).start()
    z_events(1)
    z_events(2)
    for k in range(chunks):
        cols = slice(k * wide, (k + 1) * wide)
        pre[:, cols] = dot_nn(normed[...], convf[1, :, cols])
    x_events(1)
    x_events(2)
    for k in range(chunks):
        cols = slice(k * wide, (k + 1) * wide)
        q_copy(k).wait_recv()
        v = pre[:, cols] + q_in[k].astype(jnp.float32)
        pre[:, cols] = v
        act[:, cols] = (0.5 * v * (1.0 + jnp.tanh(GELU_K * (v + GELU_C * v * v * v)))).astype(jnp.bfloat16)
    c_waits(1)
    for k in range(width // 512):
        cols = slice(k * 512, (k + 1) * 512)
        stream[:, cols] = (
            x_ref[:, cols].astype(jnp.float32) + back_dot(act[...], projf[cols, :])
        ).astype(jnp.bfloat16)
    lane = lax.broadcasted_iota(jnp.int32, (rows, LANES), 1)
    stream[:, width:] = jnp.where(lane == 0, 1.0, 0.0).astype(jnp.bfloat16)
    c_waits(2)
    logits = back_dot(stream[...], headf[...])
    expo = jnp.exp(-jnp.abs(logits))
    rate = jnp.maximum(logits, 0.0) + jnp.log1p(expo) + 0.05
    seen = counts_ref[...].astype(jnp.float32)
    terms = rate - seen * jnp.log(rate)
    losses[me] = jnp.broadcast_to(jnp.sum(terms), losses.shape[1:])
    inv = 1.0 / (1.0 + expo)
    sig = jnp.where(logits >= 0, inv, expo * inv)
    lg = ((1.0 - seen / rate) * sig).astype(jnp.bfloat16)

    def l_copy(off):
        return remote(losses.at[me], losses.at[me], l_send.at[off], l_recv.at[me], (me + off) % n)

    for off in range(1, n):
        l_copy(off).start()
    for k in range(width // 512):
        cols = slice(k * 512, (k + 1) * 512)
        part = dot_nn(lg, headf[:, cols])
        res[:, cols] = part
        normed[:, cols] = part.astype(jnp.bfloat16)
    for k in range(chunks):
        cols = slice(k * wide, (k + 1) * wide)
        ag = dot_nn(normed[...], projf[:, cols])
        v = pre[:, cols]
        th = jnp.tanh(GELU_K * (v + GELU_C * v * v * v))
        slope = 0.5 * (1.0 + th) + 0.5 * v * (1.0 - th * th) * (GELU_K * (1.0 + 3.0 * GELU_C * v * v))
        pg[k] = (ag * slope).astype(jnp.bfloat16)
        g_copy(k).start()
    for k in range(width // 512):
        cols = slice(k * 512, (k + 1) * 512)
        total = back_dot(pg[0], convf[1, cols, :wide])
        for j in range(1, chunks):
            total = total + back_dot(pg[j], convf[1, cols, j * wide:(j + 1) * wide])
        ng[:, cols] = total
    for j in range(chunks):
        g_copy(j).wait_recv()
        for k in range(width // 512):
            cols = slice(k * 512, (k + 1) * 512)
            ng[:, cols] += back_dot(pg_in[j], convf[tap, cols, j * wide:(j + 1) * wide])
    xf = x_ref[...].astype(jnp.float32)
    scale = lax.rsqrt(jnp.mean(xf * xf, axis=-1, keepdims=True) + EPS)
    dy = ng[...] * gain_ref[...]
    inner_mean = jnp.mean(xf * dy, axis=-1, keepdims=True)
    out_ref[...] = (res[...] + (scale * dy - xf * (scale * scale * scale * inner_mean))).astype(jnp.bfloat16)

    for off in range(1, n):
        source = (me + off) % n
        remote(losses.at[source], losses.at[source], l_send.at[off], l_recv.at[source], source).wait_recv()
    total = losses[0]
    for k in range(1, n):
        total = total + losses[k]
    loss_ref[...] = total * (1.0 / bins_total)

    for off in range(1, n):
        l_copy(off).wait_send()
    for k in range(chunks):
        q_copy(k).wait_send()
        g_copy(k).wait_send()
    for u in range(3):
        for zs in range(nz):
            up = (z < nz - 1) & (zs <= z)
            down = (z > 0) & (zs >= z)

            @pl.when(up)
            def _():
                z_copy(u, zs, 0).wait_send()

            @pl.when(down)
            def _():
                z_copy(u, zs, 1).wait_send()

            x_copy(u, zs).wait_send()
            for xs in range(2):
                c_copy(u, zs, xs).wait_send()


def paired(inputs, gain, conv_weight, proj_weight, head_weight, track_head_bias, counts):
    n = lax.axis_size("seq")
    seq_count, row_count, width = inputs.shape
    rows = seq_count * row_count
    tracks = counts.shape[2]
    inner = conv_weight.shape[2]
    nz = n // 4
    chunks = 3 if inner % (3 * LANES) == 0 else 1
    head_t = jnp.concatenate(
        [head_weight.T, jnp.pad(track_head_bias.T, ((0, 0), (0, LANES - 1)))], axis=1
    )
    vmem = pl.BlockSpec(memory_space=pltpu.VMEM)
    bf, f32 = jnp.bfloat16, jnp.float32
    dma = pltpu.SemaphoreType.DMA
    out, loss = pl.pallas_call(
        functools.partial(block_kernel, n, rows * n * tracks),
        out_shape=(
            jax.ShapeDtypeStruct((rows, width), bf),
            jax.ShapeDtypeStruct((8, LANES), f32),
        ),
        in_specs=[vmem] * 6,
        out_specs=(vmem, vmem),
        scratch_shapes=[
            pltpu.VMEM((3, conv_weight.shape[1] * n, inner), bf),
            pltpu.VMEM((width, inner), bf),
            pltpu.VMEM((tracks, width + LANES), bf),
            pltpu.VMEM((rows, width), bf),
            pltpu.VMEM((chunks, rows, inner // chunks), bf),
            pltpu.VMEM((chunks, rows, inner // chunks), bf),
            pltpu.VMEM((rows, inner), f32),
            pltpu.VMEM((rows, inner), bf),
            pltpu.VMEM((rows, width + LANES), bf),
            pltpu.VMEM((rows, width), f32),
            pltpu.VMEM((chunks, rows, inner // chunks), bf),
            pltpu.VMEM((chunks, rows, inner // chunks), bf),
            pltpu.VMEM((rows, width), f32),
            pltpu.VMEM((n, 8, LANES), f32),
            dma((3, nz, 2)), dma((3, nz)), dma((3, nz)), dma((3, nz)),
            dma((3, nz, 2)), dma((3, nz, 2)),
            dma((chunks,)), dma((chunks,)), dma((chunks,)), dma((chunks,)),
            dma((n,)), dma((n,)),
        ],
        compiler_params=pltpu.CompilerParams(
            collective_id=0, has_side_effects=True, vmem_limit_bytes=58 * 1024 * 1024
        ),
    )(
        inputs.reshape(rows, width), gain.reshape(1, width), conv_weight, proj_weight.T,
        head_t, counts.reshape(rows, tracks),
    )
    return out.reshape(inputs.shape), loss[0, :1]


def fits(mesh, conv_weight, proj_weight, head_weight, inputs):
    n = mesh.shape["seq"]
    shard = conv_weight.shape[1] // n
    return (
        n == 2 * SPAN
        and shard % 16 == 0
        and (head_weight.shape[1] // n) % 16 == 0
        and inputs.shape[2] % 512 == 0
        and head_weight.shape[1] <= 1024
    )


def solution(mesh):
    placed = (
        P("grp", "seq", None),
        P(),
        P(None, "seq", None),
        P(None, "seq"),
        P(None, "seq"),
        P(None, "seq"),
        P("grp", "seq", None),
    )

    def run(inputs, gain, conv_weight, proj_weight, head_weight, track_head_bias, counts):
        whole = fits(mesh, conv_weight, proj_weight, head_weight, inputs)
        return jax.shard_map(
            paired if whole else shards,
            mesh=mesh,
            in_specs=placed,
            out_specs=(P("grp", "seq", None), P("grp")),
            check_vma=False,
        )(inputs, gain, conv_weight, proj_weight, head_weight, track_head_bias, counts)

    return run
```

```python
import functools

import jax
import jax.experimental.pallas as pl
import jax.experimental.pallas.tpu as pltpu
import jax.numpy as jnp
from jax import lax
from jax.sharding import PartitionSpec as P

SPAN = 8
MESH = pl.DeviceIdType.MESH
LANES = 128
EPS = 1e-06
GELU_K = 0.7978845608028654
GELU_C = 0.044715


def shifted(value, axis, steps):
    count = lax.axis_size(axis)
    initial, last = (max(0, -steps), min(count, count - steps))
    return lax.ppermute(value, axis, [(source, source + steps) for source in range(initial, last)])


def norm_rows(value_entries, gain):
    scale_inv = lax.rsqrt(jnp.mean(value_entries * value_entries, axis=-1, keepdims=True) + 1e-06)
    return value_entries * scale_inv * gain


def head_block(stream, head_full, bias_full, observed):
    logits = jnp.dot(stream, head_full, preferred_element_type=jnp.float32) + bias_full.astype(
        jnp.float32
    )
    poisson_rate = jax.nn.softplus(logits) + 0.05
    observed_f = observed.astype(jnp.float32)
    loss_total = jnp.sum(poisson_rate - observed_f * jnp.log(poisson_rate))
    logit_grad = ((1.0 - observed_f / poisson_rate) * jax.nn.sigmoid(logits)).astype(jnp.bfloat16)
    residual_gradient = lax.dot_general(
        logit_grad, head_full, (((1,), (1,)), ((), ())), preferred_element_type=jnp.float32
    )
    return (loss_total, residual_gradient)


def back_dot(left, right):
    return lax.dot_general(
        left, right, (((1,), (1,)), ((), ())), preferred_element_type=jnp.float32
    )


def shards(inputs, gain, conv_weight, proj_weight, head_weight, track_head_bias, counts):
    seq_count, row_count, window_width = inputs.shape
    flat_rows = seq_count * row_count
    track_count = counts.shape[2]
    conv_full, proj_full = (
        lax.all_gather(conv_weight, "seq", axis=1, tiled=True),
        lax.all_gather(proj_weight, "seq", axis=1, tiled=True),
    )
    inner = conv_full.shape[2]
    inputs_f = inputs.astype(jnp.float32)
    normed = norm_rows(inputs_f, gain).astype(jnp.bfloat16)
    normed_flat = normed.reshape(flat_rows, window_width)
    behind_rows = shifted(normed, "seq", SPAN).reshape(flat_rows, window_width)
    ahead_rows = shifted(normed, "seq", -SPAN).reshape(flat_rows, window_width)
    conv_pre = jnp.dot(normed_flat, conv_full[1], preferred_element_type=jnp.float32)
    conv_pre = conv_pre + jnp.dot(behind_rows, conv_full[0], preferred_element_type=jnp.float32)
    conv_pre = conv_pre + jnp.dot(ahead_rows, conv_full[2], preferred_element_type=jnp.float32)
    conv_act = jax.nn.gelu(conv_pre).astype(jnp.bfloat16)
    stream = (
        inputs_f.reshape(flat_rows, window_width)
        + jnp.dot(conv_act, proj_full, preferred_element_type=jnp.float32)
    ).astype(jnp.bfloat16)
    counts_flat = counts.reshape(flat_rows, track_count)
    head_full, bias_full = (
        lax.all_gather(head_weight, "seq", axis=1, tiled=True),
        lax.all_gather(track_head_bias, "seq", axis=1, tiled=True),
    )
    loss_total, residual_gradient = head_block(stream, head_full, bias_full, counts_flat)
    summed_loss = lax.psum(loss_total, "seq")
    loss_value = (summed_loss / (flat_rows * lax.axis_size("seq") * track_count)).reshape(1)
    act_grad = back_dot(residual_gradient.astype(jnp.bfloat16), proj_full)
    _, gelu_back = jax.vjp(jax.nn.gelu, conv_pre)
    pre_grad = gelu_back(act_grad)[0].astype(jnp.bfloat16)
    pre_three = pre_grad.reshape(seq_count, row_count, inner)
    grad_ahead = shifted(pre_three, "seq", -SPAN).reshape(flat_rows, inner)
    grad_behind = shifted(pre_three, "seq", SPAN).reshape(flat_rows, inner)
    normed_grad = back_dot(pre_grad, conv_full[1])
    normed_grad = normed_grad + back_dot(grad_ahead, conv_full[0])
    normed_grad = normed_grad + back_dot(grad_behind, conv_full[2])
    _, norm_back = jax.vjp(lambda value_entries: norm_rows(value_entries, gain), inputs_f)
    input_grad = (
        residual_gradient.reshape(seq_count, row_count, window_width)
        + norm_back(normed_grad.reshape(seq_count, row_count, window_width))[0]
    ).astype(jnp.bfloat16)
    return (input_grad, loss_value)


def dot_nn(left, right):
    return jnp.dot(left, right, preferred_element_type=jnp.float32)


def block_kernel(
    n, bins_total, x_ref, gain_ref, conv_ref, proj_ref, head_ref, bias_ref, counts_ref, out_ref, loss_ref,
    convf, projf, headf, head_own, normed, q_out, q_in, pre, act, stream, res, pg, pg_in, ng, losses,
    z_send, z_recv, x_send, x_recv, y_send, y_recv, c_send, c_recv,
    q_send, q_recv, g_send, g_recv, l_send, l_recv, own_sem,
):
    me = lax.axis_index("seq")
    grp = lax.axis_index("grp")
    nz = n // 4
    half = nz // 2
    core = me % 2
    col = (me // 2) % 2
    z = me // 4
    low = z // half
    tap = 2 * low
    partner = (me + n // 2) % n
    x_peer = z * 4 + (1 - col) * 2 + core
    c_peer = z * 4 + col * 2 + (1 - core)
    rows, width = x_ref.shape
    inner = convf.shape[2]
    conv_depth = conv_ref.shape[1]
    depths = (conv_depth, conv_depth, proj_ref.shape[0], head_ref.shape[0], conv_depth)
    taps = (tap, 1, None, None, 2 - tap)
    slots = (4 * low, 1, 2, 3, 4 * (1 - low))
    can_up = ((z < nz - 1) & (z != half - 1), z < nz - 1, z < nz - 1, z < nz - 1, low == 0)
    can_down = ((z > 0) & (z != half), z > 0, z > 0, z > 0, low == 1)

    def place(u, zs, xs, cs):
        start = pl.multiple_of((zs * 4 + xs * 2 + cs) * depths[u], depths[u])
        if u == 2:
            return projf.at[pl.ds(start, depths[u]), :]
        if u == 3:
            return headf.at[pl.ds(start, depths[u]), :]
        return convf.at[taps[u], pl.ds(start, depths[u]), :]

    def mine(u):
        if u == 2:
            return proj_ref
        if u == 3:
            return head_own
        return conv_ref.at[taps[u]]

    def remote(src, dst, send, recv, target):
        return pltpu.make_async_remote_copy(
            src_ref=src, dst_ref=dst, send_sem=send, recv_sem=recv,
            device_id={"seq": target}, device_id_type=MESH,
        )

    def z_copy(u, zs, way, own=False):
        dst = place(u, zs, col, core)
        src = mine(u) if own else dst
        target = me + (4 if way == 0 else -4)
        return remote(src, dst, z_send.at[slots[u], zs, way], z_recv.at[slots[u], zs], target)

    def x_copy(u, zs, own=False):
        dst = place(u, zs, col, core)
        src = mine(u) if own else dst
        return remote(src, dst, x_send.at[u, zs], x_recv.at[u, zs], x_peer)

    def y_copy(u, zs):
        dst = place(u, zs, 1 - col, core)
        return pltpu.make_async_remote_copy(
            src_ref=dst, dst_ref=dst, send_sem=y_send.at[u, zs], recv_sem=y_recv.at[u, zs],
            device_id={"grp": 1 - grp}, device_id_type=MESH,
        )

    def c_copy(u, zs, xs, own=False):
        dst = place(u, zs, xs, core)
        src = mine(u) if own else dst
        return remote(src, dst, c_send.at[u, zs, xs], c_recv.at[u, zs, xs], c_peer)

    def spread(u, zs, own=False):
        @pl.when(zs % 2 == grp)
        def _():
            x_copy(u, zs, own).start()

        c_copy(u, zs, col, own).start()

    def own_sends(u):
        @pl.when(can_up[u])
        def _():
            z_copy(u, z, 0, True).start()

        @pl.when(can_down[u])
        def _():
            z_copy(u, z, 1, True).start()

        if u != 4:
            spread(u, z, True)

    def z_events(u):
        for step in range(1, nz):
            @pl.when((z - step >= 0) if u != 4 else (z - step >= 0) & (low == 0))
            def _():
                zs = z - step
                z_copy(u, zs, 0).wait_recv()

                @pl.when(can_up[u])
                def _():
                    z_copy(u, zs, 0).start()

                if u != 4:
                    spread(u, zs)

            @pl.when((z + step < nz) if u != 4 else (z + step < nz) & (low == 1))
            def _():
                zs = z + step
                z_copy(u, zs, 1).wait_recv()

                @pl.when(can_down[u])
                def _():
                    z_copy(u, zs, 1).start()

                if u != 4:
                    spread(u, zs)

    def x_events(u):
        for step in range(nz):
            zs = 2 * ((z // 2 + step // 2) % (nz // 2)) + (z % 2 + step % 2) % 2
            dst = place(u, zs, 1 - col, core)

            @pl.when(zs % 2 == grp)
            def _():
                remote(dst, dst, x_send.at[u, zs], x_recv.at[u, zs], x_peer).wait_recv()
                y_copy(u, zs).start()

            @pl.when(zs % 2 != grp)
            def _():
                y_copy(u, zs).wait_recv()

            c_copy(u, zs, 1 - col).start()

    def c_waits(u):
        for xs in range(2):
            for zs in range(nz):
                dst = place(u, zs, xs, 1 - core)
                remote(dst, dst, c_send.at[u, zs, xs], c_recv.at[u, zs, xs], c_peer).wait_recv()

    fill = [
        pltpu.make_async_copy(head_ref, head_own.at[:, pl.ds(0, width)], own_sem.at[0]),
        pltpu.make_async_copy(bias_ref, head_own.at[:, pl.ds(width, LANES)], own_sem.at[1]),
    ]
    for copy in fill:
        copy.start()
    barrier = pltpu.get_barrier_semaphore()
    for off in range(1, n):
        pl.semaphore_signal(barrier, inc=1, device_id={"seq": (me + off) % n}, device_id_type=MESH)
    pl.semaphore_signal(barrier, inc=1, device_id={"grp": 1 - grp}, device_id_type=MESH)
    pl.semaphore_wait(barrier, n)

    own_sends(0)
    own_sends(4)
    own_sends(1)
    for copy in fill:
        copy.wait()
    rows_of = [pl.ds(pl.multiple_of(me * depths[u], depths[u]), depths[u]) for u in range(4)]
    convf[tap, rows_of[0], :] = conv_ref[tap]
    convf[1, rows_of[1], :] = conv_ref[1]
    projf[rows_of[2], :] = proj_ref[...]
    headf[rows_of[3], :] = head_own[...]
    xf = x_ref[...].astype(jnp.float32)
    scale = lax.rsqrt(jnp.mean(xf * xf, axis=-1, keepdims=True) + EPS)
    normed[...] = (xf * scale * gain_ref[...]).astype(jnp.bfloat16)
    z_events(4)
    z_events(0)
    own_sends(2)
    own_sends(3)
    z_events(1)
    x_events(0)
    z_events(2)
    c_waits(0)

    chunks = q_out.shape[0]
    wide = inner // chunks

    def q_copy(k):
        return remote(q_out.at[k], q_in.at[k], q_send.at[k], q_recv.at[k], partner)

    def g_copy(k):
        return remote(pg.at[k], pg_in.at[k], g_send.at[k], g_recv.at[k], partner)

    for k in range(chunks):
        cols = slice(k * wide, (k + 1) * wide)
        q_out[k] = dot_nn(normed[...], convf[tap, :, cols]).astype(jnp.bfloat16)
        q_copy(k).start()
    z_events(3)
    x_events(1)
    c_waits(1)
    for k in range(chunks):
        cols = slice(k * wide, (k + 1) * wide)
        pre[:, cols] = dot_nn(normed[...], convf[1, :, cols])
    x_events(2)
    x_events(3)
    for k in range(chunks):
        cols = slice(k * wide, (k + 1) * wide)
        q_copy(k).wait_recv()
        v = pre[:, cols] + q_in[k].astype(jnp.float32)
        pre[:, cols] = v
        act[:, cols] = (0.5 * v * (1.0 + jnp.tanh(GELU_K * (v + GELU_C * v * v * v)))).astype(jnp.bfloat16)
    c_waits(2)
    for k in range(width // 512):
        cols = slice(k * 512, (k + 1) * 512)
        stream[:, cols] = (
            x_ref[:, cols].astype(jnp.float32) + back_dot(act[...], projf[cols, :])
        ).astype(jnp.bfloat16)
    lane = lax.broadcasted_iota(jnp.int32, (rows, LANES), 1)
    stream[:, width:] = jnp.where(lane == 0, 1.0, 0.0).astype(jnp.bfloat16)
    c_waits(3)
    logits = back_dot(stream[...], headf[...])
    expo = jnp.exp(-jnp.abs(logits))
    rate = jnp.maximum(logits, 0.0) + jnp.log1p(expo) + 0.05
    seen = counts_ref[...].astype(jnp.float32)
    terms = rate - seen * jnp.log(rate)
    losses[me] = jnp.broadcast_to(jnp.sum(terms), losses.shape[1:])
    inv = 1.0 / (1.0 + expo)
    sig = jnp.where(logits >= 0, inv, expo * inv)
    lg = ((1.0 - seen / rate) * sig).astype(jnp.bfloat16)

    def l_copy(off):
        return remote(losses.at[me], losses.at[me], l_send.at[off], l_recv.at[me], (me + off) % n)

    for off in range(1, n):
        l_copy(off).start()
    for k in range(width // 512):
        cols = slice(k * 512, (k + 1) * 512)
        part = dot_nn(lg, headf[:, cols])
        res[:, cols] = part
        normed[:, cols] = part.astype(jnp.bfloat16)
    for k in range(chunks):
        cols = slice(k * wide, (k + 1) * wide)
        ag = dot_nn(normed[...], projf[:, cols])
        v = pre[:, cols]
        th = jnp.tanh(GELU_K * (v + GELU_C * v * v * v))
        slope = 0.5 * (1.0 + th) + 0.5 * v * (1.0 - th * th) * (GELU_K * (1.0 + 3.0 * GELU_C * v * v))
        pg[k] = (ag * slope).astype(jnp.bfloat16)
        g_copy(k).start()
    for k in range(width // 512):
        cols = slice(k * 512, (k + 1) * 512)
        total = back_dot(pg[0], convf[1, cols, :wide])
        for j in range(1, chunks):
            total = total + back_dot(pg[j], convf[1, cols, j * wide:(j + 1) * wide])
        ng[:, cols] = total
    for j in range(chunks):
        g_copy(j).wait_recv()
        for k in range(width // 512):
            cols = slice(k * 512, (k + 1) * 512)
            ng[:, cols] += back_dot(pg_in[j], convf[tap, cols, j * wide:(j + 1) * wide])
    xf = x_ref[...].astype(jnp.float32)
    scale = lax.rsqrt(jnp.mean(xf * xf, axis=-1, keepdims=True) + EPS)
    dy = ng[...] * gain_ref[...]
    inner_mean = jnp.mean(xf * dy, axis=-1, keepdims=True)
    out_ref[...] = (res[...] + (scale * dy - xf * (scale * scale * scale * inner_mean))).astype(jnp.bfloat16)

    for off in range(1, n):
        source = (me + off) % n
        remote(losses.at[source], losses.at[source], l_send.at[off], l_recv.at[source], source).wait_recv()
    total = losses[0]
    for k in range(1, n):
        total = total + losses[k]
    loss_ref[0] = total[0, 0] * (1.0 / bins_total)

    for off in range(1, n):
        l_copy(off).wait_send()
    for k in range(chunks):
        q_copy(k).wait_send()
        g_copy(k).wait_send()
    for u in range(5):
        for zs in range(nz):
            @pl.when(can_up[u] & (zs <= z))
            def _():
                z_copy(u, zs, 0).wait_send()

            @pl.when(can_down[u] & (zs >= z))
            def _():
                z_copy(u, zs, 1).wait_send()

            if u != 4:
                @pl.when(zs % 2 == grp)
                def _():
                    x_copy(u, zs).wait_send()
                    y_copy(u, zs).wait_send()

                for xs in range(2):
                    c_copy(u, zs, xs).wait_send()


def paired(inputs, gain, conv_weight, proj_weight, head_weight, track_head_bias, counts):
    n = lax.axis_size("seq")
    seq_count, row_count, width = inputs.shape
    rows = seq_count * row_count
    tracks = counts.shape[2]
    inner = conv_weight.shape[2]
    nz = n // 4
    chunks = 3 if inner % (3 * LANES) == 0 else 1
    bias_t = jnp.pad(track_head_bias.T, ((0, 0), (0, LANES - 1)))
    vmem = pl.BlockSpec(memory_space=pltpu.VMEM)
    bf, f32 = jnp.bfloat16, jnp.float32
    dma = pltpu.SemaphoreType.DMA
    out, loss = pl.pallas_call(
        functools.partial(block_kernel, n, rows * n * tracks),
        out_shape=(
            jax.ShapeDtypeStruct((rows, width), bf),
            jax.ShapeDtypeStruct((1,), f32),
        ),
        in_specs=[vmem] * 7,
        out_specs=(vmem, pl.BlockSpec(memory_space=pltpu.SMEM)),
        scratch_shapes=[
            pltpu.VMEM((3, conv_weight.shape[1] * n, inner), bf),
            pltpu.VMEM((width, inner), bf),
            pltpu.VMEM((tracks, width + LANES), bf),
            pltpu.VMEM((tracks // n, width + LANES), bf),
            pltpu.VMEM((rows, width), bf),
            pltpu.VMEM((chunks, rows, inner // chunks), bf),
            pltpu.VMEM((chunks, rows, inner // chunks), bf),
            pltpu.VMEM((rows, inner), f32),
            pltpu.VMEM((rows, inner), bf),
            pltpu.VMEM((rows, width + LANES), bf),
            pltpu.VMEM((rows, width), f32),
            pltpu.VMEM((chunks, rows, inner // chunks), bf),
            pltpu.VMEM((chunks, rows, inner // chunks), bf),
            pltpu.VMEM((rows, width), f32),
            pltpu.VMEM((n, 8, LANES), f32),
            dma((5, nz, 2)), dma((5, nz)), dma((4, nz)), dma((4, nz)),
            dma((4, nz)), dma((4, nz)), dma((4, nz, 2)), dma((4, nz, 2)),
            dma((chunks,)), dma((chunks,)), dma((chunks,)), dma((chunks,)),
            dma((n,)), dma((n,)), dma((2,)),
        ],
        compiler_params=pltpu.CompilerParams(
            collective_id=0, has_side_effects=True, vmem_limit_bytes=58 * 1024 * 1024
        ),
    )(
        inputs.reshape(rows, width), gain.reshape(1, width), conv_weight, proj_weight.T,
        head_weight.T, bias_t, counts.reshape(rows, tracks),
    )
    return out.reshape(inputs.shape), loss


def fits(mesh, conv_weight, proj_weight, head_weight, inputs):
    n = mesh.shape["seq"]
    shard = conv_weight.shape[1] // n
    return (
        n == 2 * SPAN
        and mesh.shape["grp"] == 2
        and shard % 16 == 0
        and (head_weight.shape[1] // n) % 16 == 0
        and inputs.shape[2] % 512 == 0
        and head_weight.shape[1] <= 1024
    )


def solution(mesh):
    placed = (
        P("grp", "seq", None),
        P(),
        P(None, "seq", None),
        P(None, "seq"),
        P(None, "seq"),
        P(None, "seq"),
        P("grp", "seq", None),
    )

    def run(inputs, gain, conv_weight, proj_weight, head_weight, track_head_bias, counts):
        whole = fits(mesh, conv_weight, proj_weight, head_weight, inputs)
        return jax.shard_map(
            paired if whole else shards,
            mesh=mesh,
            in_specs=placed,
            out_specs=(P("grp", "seq", None), P("grp")),
            check_vma=False,
        )(inputs, gain, conv_weight, proj_weight, head_weight, track_head_bias, counts)

    return run
```

```python
import functools

import jax
import jax.experimental.pallas as pl
import jax.experimental.pallas.tpu as pltpu
import jax.numpy as jnp
from jax import lax
from jax.sharding import PartitionSpec as P

SPAN = 8
MESH = pl.DeviceIdType.MESH
LANES = 128
EPS = 1e-06
GELU_K = 0.7978845608028654
GELU_C = 0.044715


def shifted(value, axis, steps):
    count = lax.axis_size(axis)
    initial, last = (max(0, -steps), min(count, count - steps))
    return lax.ppermute(value, axis, [(source, source + steps) for source in range(initial, last)])


def norm_rows(value_entries, gain):
    scale_inv = lax.rsqrt(jnp.mean(value_entries * value_entries, axis=-1, keepdims=True) + 1e-06)
    return value_entries * scale_inv * gain


def head_block(stream, head_full, bias_full, observed):
    logits = jnp.dot(stream, head_full, preferred_element_type=jnp.float32) + bias_full.astype(
        jnp.float32
    )
    poisson_rate = jax.nn.softplus(logits) + 0.05
    observed_f = observed.astype(jnp.float32)
    loss_total = jnp.sum(poisson_rate - observed_f * jnp.log(poisson_rate))
    logit_grad = ((1.0 - observed_f / poisson_rate) * jax.nn.sigmoid(logits)).astype(jnp.bfloat16)
    residual_gradient = lax.dot_general(
        logit_grad, head_full, (((1,), (1,)), ((), ())), preferred_element_type=jnp.float32
    )
    return (loss_total, residual_gradient)


def back_dot(left, right):
    return lax.dot_general(
        left, right, (((1,), (1,)), ((), ())), preferred_element_type=jnp.float32
    )


def shards(inputs, gain, conv_weight, proj_weight, head_weight, track_head_bias, counts):
    seq_count, row_count, window_width = inputs.shape
    flat_rows = seq_count * row_count
    track_count = counts.shape[2]
    conv_full, proj_full = (
        lax.all_gather(conv_weight, "seq", axis=1, tiled=True),
        lax.all_gather(proj_weight, "seq", axis=1, tiled=True),
    )
    inner = conv_full.shape[2]
    inputs_f = inputs.astype(jnp.float32)
    normed = norm_rows(inputs_f, gain).astype(jnp.bfloat16)
    normed_flat = normed.reshape(flat_rows, window_width)
    behind_rows = shifted(normed, "seq", SPAN).reshape(flat_rows, window_width)
    ahead_rows = shifted(normed, "seq", -SPAN).reshape(flat_rows, window_width)
    conv_pre = jnp.dot(normed_flat, conv_full[1], preferred_element_type=jnp.float32)
    conv_pre = conv_pre + jnp.dot(behind_rows, conv_full[0], preferred_element_type=jnp.float32)
    conv_pre = conv_pre + jnp.dot(ahead_rows, conv_full[2], preferred_element_type=jnp.float32)
    conv_act = jax.nn.gelu(conv_pre).astype(jnp.bfloat16)
    stream = (
        inputs_f.reshape(flat_rows, window_width)
        + jnp.dot(conv_act, proj_full, preferred_element_type=jnp.float32)
    ).astype(jnp.bfloat16)
    counts_flat = counts.reshape(flat_rows, track_count)
    head_full, bias_full = (
        lax.all_gather(head_weight, "seq", axis=1, tiled=True),
        lax.all_gather(track_head_bias, "seq", axis=1, tiled=True),
    )
    loss_total, residual_gradient = head_block(stream, head_full, bias_full, counts_flat)
    summed_loss = lax.psum(loss_total, "seq")
    loss_value = (summed_loss / (flat_rows * lax.axis_size("seq") * track_count)).reshape(1)
    act_grad = back_dot(residual_gradient.astype(jnp.bfloat16), proj_full)
    _, gelu_back = jax.vjp(jax.nn.gelu, conv_pre)
    pre_grad = gelu_back(act_grad)[0].astype(jnp.bfloat16)
    pre_three = pre_grad.reshape(seq_count, row_count, inner)
    grad_ahead = shifted(pre_three, "seq", -SPAN).reshape(flat_rows, inner)
    grad_behind = shifted(pre_three, "seq", SPAN).reshape(flat_rows, inner)
    normed_grad = back_dot(pre_grad, conv_full[1])
    normed_grad = normed_grad + back_dot(grad_ahead, conv_full[0])
    normed_grad = normed_grad + back_dot(grad_behind, conv_full[2])
    _, norm_back = jax.vjp(lambda value_entries: norm_rows(value_entries, gain), inputs_f)
    input_grad = (
        residual_gradient.reshape(seq_count, row_count, window_width)
        + norm_back(normed_grad.reshape(seq_count, row_count, window_width))[0]
    ).astype(jnp.bfloat16)
    return (input_grad, loss_value)


def dot_nn(left, right):
    return jnp.dot(left, right, preferred_element_type=jnp.float32)


def block_kernel(
    n, bins_total, x_ref, gain_ref, conv_ref, proj_ref, head_ref, bias_ref, counts_ref, out_ref, loss_ref,
    convf, projf, headf, head_own, normed, q_out, q_in, pre, act, stream, res, pg, pg_in, ng, losses,
    z_send, z_recv, x_send, x_recv, y_send, y_recv, c_send, c_recv,
    q_send, q_recv, g_send, g_recv, l_send, l_recv, own_sem,
):
    me = lax.axis_index("seq")
    grp = lax.axis_index("grp")
    nz = n // 4
    half = nz // 2
    core = me % 2
    col = (me // 2) % 2
    z = me // 4
    low = z // half
    tap = 2 * low
    partner = (me + n // 2) % n
    x_peer = z * 4 + (1 - col) * 2 + core
    c_peer = z * 4 + col * 2 + (1 - core)
    rows, width = x_ref.shape
    inner = convf.shape[2]
    conv_depth = conv_ref.shape[1]
    depths = (conv_depth, conv_depth, proj_ref.shape[0], head_ref.shape[0], conv_depth)
    taps = (tap, 1, None, None, 2 - tap)
    slots = (4 * low, 1, 2, 3, 4 * (1 - low))
    can_up = ((z < nz - 1) & (z != half - 1), z < nz - 1, z < nz - 1, z < nz - 1, low == 0)
    can_down = ((z > 0) & (z != half), z > 0, z > 0, z > 0, low == 1)

    def place(u, zs, xs, cs):
        start = pl.multiple_of((zs * 4 + xs * 2 + cs) * depths[u], depths[u])
        if u == 2:
            return projf.at[pl.ds(start, depths[u]), :]
        if u == 3:
            return headf.at[pl.ds(start, depths[u]), :]
        return convf.at[taps[u], pl.ds(start, depths[u]), :]

    def mine(u):
        if u == 2:
            return proj_ref
        if u == 3:
            return head_own
        return conv_ref.at[taps[u]]

    def remote(src, dst, send, recv, target):
        return pltpu.make_async_remote_copy(
            src_ref=src, dst_ref=dst, send_sem=send, recv_sem=recv,
            device_id={"seq": target}, device_id_type=MESH,
        )

    def z_copy(u, zs, way, own=False):
        dst = place(u, zs, col, core)
        src = mine(u) if own else dst
        target = me + (4 if way == 0 else -4)
        return remote(src, dst, z_send.at[slots[u], zs, way], z_recv.at[slots[u], zs], target)

    def x_copy(u, zs, own=False):
        dst = place(u, zs, col, core)
        src = mine(u) if own else dst
        return remote(src, dst, x_send.at[u, zs], x_recv.at[u, zs], x_peer)

    def y_copy(u, zs):
        dst = place(u, zs, 1 - col, core)
        return pltpu.make_async_remote_copy(
            src_ref=dst, dst_ref=dst, send_sem=y_send.at[u, zs], recv_sem=y_recv.at[u, zs],
            device_id={"grp": 1 - grp}, device_id_type=MESH,
        )

    def c_copy(u, zs, xs, own=False):
        dst = place(u, zs, xs, core)
        src = mine(u) if own else dst
        return remote(src, dst, c_send.at[u, zs, xs], c_recv.at[u, zs, xs], c_peer)

    def spread(u, zs, own=False):
        x_copy(u, zs, own).start()

        c_copy(u, zs, col, own).start()

    def own_sends(u):
        @pl.when(can_up[u])
        def _():
            z_copy(u, z, 0, True).start()

        @pl.when(can_down[u])
        def _():
            z_copy(u, z, 1, True).start()

        if u != 4:
            spread(u, z, True)

    def z_events(u):
        for step in range(1, nz):
            @pl.when((z - step >= 0) if u != 4 else (z - step >= 0) & (low == 0))
            def _():
                zs = z - step
                z_copy(u, zs, 0).wait_recv()

                @pl.when(can_up[u])
                def _():
                    z_copy(u, zs, 0).start()

                if u != 4:
                    spread(u, zs)

            @pl.when((z + step < nz) if u != 4 else (z + step < nz) & (low == 1))
            def _():
                zs = z + step
                z_copy(u, zs, 1).wait_recv()

                @pl.when(can_down[u])
                def _():
                    z_copy(u, zs, 1).start()

                if u != 4:
                    spread(u, zs)

    def x_events(u):
        for step in range(nz):
            zs = 2 * ((z // 2 + step // 2) % (nz // 2)) + (z % 2 + step % 2) % 2
            dst = place(u, zs, 1 - col, core)

            remote(dst, dst, x_send.at[u, zs], x_recv.at[u, zs], x_peer).wait_recv()
            c_copy(u, zs, 1 - col).start()

    def c_waits(u):
        for xs in range(2):
            for zs in range(nz):
                dst = place(u, zs, xs, 1 - core)
                remote(dst, dst, c_send.at[u, zs, xs], c_recv.at[u, zs, xs], c_peer).wait_recv()

    fill = [
        pltpu.make_async_copy(head_ref, head_own.at[:, pl.ds(0, width)], own_sem.at[0]),
        pltpu.make_async_copy(bias_ref, head_own.at[:, pl.ds(width, LANES)], own_sem.at[1]),
    ]
    for copy in fill:
        copy.start()
    barrier = pltpu.get_barrier_semaphore()
    for off in range(1, n):
        pl.semaphore_signal(barrier, inc=1, device_id={"seq": (me + off) % n}, device_id_type=MESH)
    pl.semaphore_signal(barrier, inc=1, device_id={"grp": 1 - grp}, device_id_type=MESH)
    pl.semaphore_wait(barrier, n)

    own_sends(0)
    own_sends(4)
    own_sends(1)
    for copy in fill:
        copy.wait()
    rows_of = [pl.ds(pl.multiple_of(me * depths[u], depths[u]), depths[u]) for u in range(4)]
    convf[tap, rows_of[0], :] = conv_ref[tap]
    convf[1, rows_of[1], :] = conv_ref[1]
    projf[rows_of[2], :] = proj_ref[...]
    headf[rows_of[3], :] = head_own[...]
    xf = x_ref[...].astype(jnp.float32)
    scale = lax.rsqrt(jnp.mean(xf * xf, axis=-1, keepdims=True) + EPS)
    normed[...] = (xf * scale * gain_ref[...]).astype(jnp.bfloat16)
    z_events(4)
    z_events(0)
    own_sends(2)
    own_sends(3)
    z_events(1)
    x_events(0)
    z_events(2)
    c_waits(0)

    chunks = q_out.shape[0]
    wide = inner // chunks

    def q_copy(k):
        return remote(q_out.at[k], q_in.at[k], q_send.at[k], q_recv.at[k], partner)

    def g_copy(k):
        return remote(pg.at[k], pg_in.at[k], g_send.at[k], g_recv.at[k], partner)

    for k in range(chunks):
        cols = slice(k * wide, (k + 1) * wide)
        q_out[k] = dot_nn(normed[...], convf[tap, :, cols]).astype(jnp.bfloat16)
        q_copy(k).start()
    z_events(3)
    x_events(1)
    c_waits(1)
    for k in range(chunks):
        cols = slice(k * wide, (k + 1) * wide)
        pre[:, cols] = dot_nn(normed[...], convf[1, :, cols])
    x_events(2)
    x_events(3)
    for k in range(chunks):
        cols = slice(k * wide, (k + 1) * wide)
        q_copy(k).wait_recv()
        v = pre[:, cols] + q_in[k].astype(jnp.float32)
        pre[:, cols] = v
        act[:, cols] = (0.5 * v * (1.0 + jnp.tanh(GELU_K * (v + GELU_C * v * v * v)))).astype(jnp.bfloat16)
    c_waits(2)
    for k in range(width // 512):
        cols = slice(k * 512, (k + 1) * 512)
        stream[:, cols] = (
            x_ref[:, cols].astype(jnp.float32) + back_dot(act[...], projf[cols, :])
        ).astype(jnp.bfloat16)
    lane = lax.broadcasted_iota(jnp.int32, (rows, LANES), 1)
    stream[:, width:] = jnp.where(lane == 0, 1.0, 0.0).astype(jnp.bfloat16)
    c_waits(3)
    logits = back_dot(stream[...], headf[...])
    expo = jnp.exp(-jnp.abs(logits))
    rate = jnp.maximum(logits, 0.0) + jnp.log1p(expo) + 0.05
    seen = counts_ref[...].astype(jnp.float32)
    terms = rate - seen * jnp.log(rate)
    losses[me] = jnp.broadcast_to(jnp.sum(terms), losses.shape[1:])
    inv = 1.0 / (1.0 + expo)
    sig = jnp.where(logits >= 0, inv, expo * inv)
    lg = ((1.0 - seen / rate) * sig).astype(jnp.bfloat16)

    def l_copy(off):
        return remote(losses.at[me], losses.at[me], l_send.at[off], l_recv.at[me], (me + off) % n)

    for off in range(1, n):
        l_copy(off).start()
    for k in range(width // 512):
        cols = slice(k * 512, (k + 1) * 512)
        part = dot_nn(lg, headf[:, cols])
        res[:, cols] = part
        normed[:, cols] = part.astype(jnp.bfloat16)
    for k in range(chunks):
        cols = slice(k * wide, (k + 1) * wide)
        ag = dot_nn(normed[...], projf[:, cols])
        v = pre[:, cols]
        th = jnp.tanh(GELU_K * (v + GELU_C * v * v * v))
        slope = 0.5 * (1.0 + th) + 0.5 * v * (1.0 - th * th) * (GELU_K * (1.0 + 3.0 * GELU_C * v * v))
        pg[k] = (ag * slope).astype(jnp.bfloat16)
        g_copy(k).start()
    for k in range(width // 512):
        cols = slice(k * 512, (k + 1) * 512)
        total = back_dot(pg[0], convf[1, cols, :wide])
        for j in range(1, chunks):
            total = total + back_dot(pg[j], convf[1, cols, j * wide:(j + 1) * wide])
        ng[:, cols] = total
    for j in range(chunks):
        g_copy(j).wait_recv()
        for k in range(width // 512):
            cols = slice(k * 512, (k + 1) * 512)
            ng[:, cols] += back_dot(pg_in[j], convf[tap, cols, j * wide:(j + 1) * wide])
    xf = x_ref[...].astype(jnp.float32)
    scale = lax.rsqrt(jnp.mean(xf * xf, axis=-1, keepdims=True) + EPS)
    dy = ng[...] * gain_ref[...]
    inner_mean = jnp.mean(xf * dy, axis=-1, keepdims=True)
    out_ref[...] = (res[...] + (scale * dy - xf * (scale * scale * scale * inner_mean))).astype(jnp.bfloat16)

    for off in range(1, n):
        source = (me + off) % n
        remote(losses.at[source], losses.at[source], l_send.at[off], l_recv.at[source], source).wait_recv()
    total = losses[0]
    for k in range(1, n):
        total = total + losses[k]
    loss_ref[0] = total[0, 0] * (1.0 / bins_total)

    for off in range(1, n):
        l_copy(off).wait_send()
    for k in range(chunks):
        q_copy(k).wait_send()
        g_copy(k).wait_send()
    for u in range(5):
        for zs in range(nz):
            @pl.when(can_up[u] & (zs <= z))
            def _():
                z_copy(u, zs, 0).wait_send()

            @pl.when(can_down[u] & (zs >= z))
            def _():
                z_copy(u, zs, 1).wait_send()

            if u != 4:
                x_copy(u, zs).wait_send()

                for xs in range(2):
                    c_copy(u, zs, xs).wait_send()


def paired(inputs, gain, conv_weight, proj_weight, head_weight, track_head_bias, counts):
    n = lax.axis_size("seq")
    seq_count, row_count, width = inputs.shape
    rows = seq_count * row_count
    tracks = counts.shape[2]
    inner = conv_weight.shape[2]
    nz = n // 4
    chunks = 3 if inner % (3 * LANES) == 0 else 1
    bias_t = jnp.pad(track_head_bias.T, ((0, 0), (0, LANES - 1)))
    vmem = pl.BlockSpec(memory_space=pltpu.VMEM)
    bf, f32 = jnp.bfloat16, jnp.float32
    dma = pltpu.SemaphoreType.DMA
    out, loss = pl.pallas_call(
        functools.partial(block_kernel, n, rows * n * tracks),
        out_shape=(
            jax.ShapeDtypeStruct((rows, width), bf),
            jax.ShapeDtypeStruct((1,), f32),
        ),
        in_specs=[vmem] * 7,
        out_specs=(vmem, pl.BlockSpec(memory_space=pltpu.SMEM)),
        scratch_shapes=[
            pltpu.VMEM((3, conv_weight.shape[1] * n, inner), bf),
            pltpu.VMEM((width, inner), bf),
            pltpu.VMEM((tracks, width + LANES), bf),
            pltpu.VMEM((tracks // n, width + LANES), bf),
            pltpu.VMEM((rows, width), bf),
            pltpu.VMEM((chunks, rows, inner // chunks), bf),
            pltpu.VMEM((chunks, rows, inner // chunks), bf),
            pltpu.VMEM((rows, inner), f32),
            pltpu.VMEM((rows, inner), bf),
            pltpu.VMEM((rows, width + LANES), bf),
            pltpu.VMEM((rows, width), f32),
            pltpu.VMEM((chunks, rows, inner // chunks), bf),
            pltpu.VMEM((chunks, rows, inner // chunks), bf),
            pltpu.VMEM((rows, width), f32),
            pltpu.VMEM((n, 8, LANES), f32),
            dma((5, nz, 2)), dma((5, nz)), dma((4, nz)), dma((4, nz)),
            dma((4, nz)), dma((4, nz)), dma((4, nz, 2)), dma((4, nz, 2)),
            dma((chunks,)), dma((chunks,)), dma((chunks,)), dma((chunks,)),
            dma((n,)), dma((n,)), dma((2,)),
        ],
        compiler_params=pltpu.CompilerParams(
            collective_id=0, has_side_effects=True, vmem_limit_bytes=58 * 1024 * 1024
        ),
    )(
        inputs.reshape(rows, width), gain.reshape(1, width), conv_weight, proj_weight.T,
        head_weight.T, bias_t, counts.reshape(rows, tracks),
    )
    return out.reshape(inputs.shape), loss


def fits(mesh, conv_weight, proj_weight, head_weight, inputs):
    n = mesh.shape["seq"]
    shard = conv_weight.shape[1] // n
    return (
        n == 2 * SPAN
        and mesh.shape["grp"] == 2
        and shard % 16 == 0
        and (head_weight.shape[1] // n) % 16 == 0
        and inputs.shape[2] % 512 == 0
        and head_weight.shape[1] <= 1024
    )


def solution(mesh):
    placed = (
        P("grp", "seq", None),
        P(),
        P(None, "seq", None),
        P(None, "seq"),
        P(None, "seq"),
        P(None, "seq"),
        P("grp", "seq", None),
    )

    def run(inputs, gain, conv_weight, proj_weight, head_weight, track_head_bias, counts):
        whole = fits(mesh, conv_weight, proj_weight, head_weight, inputs)
        return jax.shard_map(
            paired if whole else shards,
            mesh=mesh,
            in_specs=placed,
            out_specs=(P("grp", "seq", None), P("grp")),
            check_vma=False,
        )(inputs, gain, conv_weight, proj_weight, head_weight, track_head_bias, counts)

    return run
```

```python
import functools

import jax
import jax.experimental.pallas as pl
import jax.experimental.pallas.tpu as pltpu
import jax.numpy as jnp
from jax import lax
from jax.sharding import PartitionSpec as P

SPAN = 8
MESH = pl.DeviceIdType.MESH
LANES = 128
EPS = 1e-06
GELU_K = 0.7978845608028654
GELU_C = 0.044715


def shifted(value, axis, steps):
    count = lax.axis_size(axis)
    initial, last = (max(0, -steps), min(count, count - steps))
    return lax.ppermute(value, axis, [(source, source + steps) for source in range(initial, last)])


def norm_rows(value_entries, gain):
    scale_inv = lax.rsqrt(jnp.mean(value_entries * value_entries, axis=-1, keepdims=True) + 1e-06)
    return value_entries * scale_inv * gain


def head_block(stream, head_full, bias_full, observed):
    logits = jnp.dot(stream, head_full, preferred_element_type=jnp.float32) + bias_full.astype(
        jnp.float32
    )
    poisson_rate = jax.nn.softplus(logits) + 0.05
    observed_f = observed.astype(jnp.float32)
    loss_total = jnp.sum(poisson_rate - observed_f * jnp.log(poisson_rate))
    logit_grad = ((1.0 - observed_f / poisson_rate) * jax.nn.sigmoid(logits)).astype(jnp.bfloat16)
    residual_gradient = lax.dot_general(
        logit_grad, head_full, (((1,), (1,)), ((), ())), preferred_element_type=jnp.float32
    )
    return (loss_total, residual_gradient)


def back_dot(left, right):
    return lax.dot_general(
        left, right, (((1,), (1,)), ((), ())), preferred_element_type=jnp.float32
    )


def shards(inputs, gain, conv_weight, proj_weight, head_weight, track_head_bias, counts):
    seq_count, row_count, window_width = inputs.shape
    flat_rows = seq_count * row_count
    track_count = counts.shape[2]
    conv_full, proj_full = (
        lax.all_gather(conv_weight, "seq", axis=1, tiled=True),
        lax.all_gather(proj_weight, "seq", axis=1, tiled=True),
    )
    inner = conv_full.shape[2]
    inputs_f = inputs.astype(jnp.float32)
    normed = norm_rows(inputs_f, gain).astype(jnp.bfloat16)
    normed_flat = normed.reshape(flat_rows, window_width)
    behind_rows = shifted(normed, "seq", SPAN).reshape(flat_rows, window_width)
    ahead_rows = shifted(normed, "seq", -SPAN).reshape(flat_rows, window_width)
    conv_pre = jnp.dot(normed_flat, conv_full[1], preferred_element_type=jnp.float32)
    conv_pre = conv_pre + jnp.dot(behind_rows, conv_full[0], preferred_element_type=jnp.float32)
    conv_pre = conv_pre + jnp.dot(ahead_rows, conv_full[2], preferred_element_type=jnp.float32)
    conv_act = jax.nn.gelu(conv_pre).astype(jnp.bfloat16)
    stream = (
        inputs_f.reshape(flat_rows, window_width)
        + jnp.dot(conv_act, proj_full, preferred_element_type=jnp.float32)
    ).astype(jnp.bfloat16)
    counts_flat = counts.reshape(flat_rows, track_count)
    head_full, bias_full = (
        lax.all_gather(head_weight, "seq", axis=1, tiled=True),
        lax.all_gather(track_head_bias, "seq", axis=1, tiled=True),
    )
    loss_total, residual_gradient = head_block(stream, head_full, bias_full, counts_flat)
    summed_loss = lax.psum(loss_total, "seq")
    loss_value = (summed_loss / (flat_rows * lax.axis_size("seq") * track_count)).reshape(1)
    act_grad = back_dot(residual_gradient.astype(jnp.bfloat16), proj_full)
    _, gelu_back = jax.vjp(jax.nn.gelu, conv_pre)
    pre_grad = gelu_back(act_grad)[0].astype(jnp.bfloat16)
    pre_three = pre_grad.reshape(seq_count, row_count, inner)
    grad_ahead = shifted(pre_three, "seq", -SPAN).reshape(flat_rows, inner)
    grad_behind = shifted(pre_three, "seq", SPAN).reshape(flat_rows, inner)
    normed_grad = back_dot(pre_grad, conv_full[1])
    normed_grad = normed_grad + back_dot(grad_ahead, conv_full[0])
    normed_grad = normed_grad + back_dot(grad_behind, conv_full[2])
    _, norm_back = jax.vjp(lambda value_entries: norm_rows(value_entries, gain), inputs_f)
    input_grad = (
        residual_gradient.reshape(seq_count, row_count, window_width)
        + norm_back(normed_grad.reshape(seq_count, row_count, window_width))[0]
    ).astype(jnp.bfloat16)
    return (input_grad, loss_value)


def dot_nn(left, right):
    return jnp.dot(left, right, preferred_element_type=jnp.float32)


def block_kernel(
    n, bins_total, x_ref, gain_ref, conv_ref, proj_ref, head_ref, bias_ref, counts_ref, out_ref, loss_ref,
    convf, projf, headf, head_own, normed, q_out, q_in, pre, act, stream, res, pg, pg_in, ng, losses,
    z_send, z_recv, x_send, x_recv, y_send, y_recv, c_send, c_recv,
    q_send, q_recv, g_send, g_recv, l_send, l_recv, own_sem,
):
    me = lax.axis_index("seq")
    grp = lax.axis_index("grp")
    nz = n // 4
    half = nz // 2
    core = me % 2
    col = (me // 2) % 2
    z = me // 4
    low = z // half
    tap = 2 * low
    partner = (me + n // 2) % n
    x_peer = z * 4 + (1 - col) * 2 + core
    c_peer = z * 4 + col * 2 + (1 - core)
    rows, width = x_ref.shape
    inner = convf.shape[2]
    conv_depth = conv_ref.shape[1]
    depths = (conv_depth, conv_depth, proj_ref.shape[0], head_ref.shape[0], conv_depth)
    taps = (tap, 1, None, None, 2 - tap)
    slots = (4 * low, 1, 2, 3, 4 * (1 - low))
    can_up = ((z < nz - 1) & (z != half - 1), z < nz - 1, z < nz - 1, z < nz - 1, low == 0)
    can_down = ((z > 0) & (z != half), z > 0, z > 0, z > 0, low == 1)

    def place(u, zs, xs, cs):
        start = pl.multiple_of((zs * 4 + xs * 2 + cs) * depths[u], depths[u])
        if u == 2:
            return projf.at[pl.ds(start, depths[u]), :]
        if u == 3:
            return headf.at[pl.ds(start, depths[u]), :]
        return convf.at[taps[u], pl.ds(start, depths[u]), :]

    def mine(u):
        if u == 2:
            return proj_ref
        if u == 3:
            return head_own
        return conv_ref.at[taps[u]]

    def remote(src, dst, send, recv, target):
        return pltpu.make_async_remote_copy(
            src_ref=src, dst_ref=dst, send_sem=send, recv_sem=recv,
            device_id={"seq": target}, device_id_type=MESH,
        )

    def z_copy(u, zs, way, own=False):
        dst = place(u, zs, col, core)
        src = mine(u) if own else dst
        target = me + (4 if way == 0 else -4)
        return remote(src, dst, z_send.at[slots[u], zs, way], z_recv.at[slots[u], zs], target)

    def x_copy(u, zs, own=False):
        dst = place(u, zs, col, core)
        src = mine(u) if own else dst
        return remote(src, dst, x_send.at[u, zs], x_recv.at[u, zs], x_peer)

    def y_copy(u, zs):
        dst = place(u, zs, 1 - col, core)
        return pltpu.make_async_remote_copy(
            src_ref=dst, dst_ref=dst, send_sem=y_send.at[u, zs], recv_sem=y_recv.at[u, zs],
            device_id={"grp": 1 - grp}, device_id_type=MESH,
        )

    def c_copy(u, zs, xs, own=False):
        dst = place(u, zs, xs, core)
        src = mine(u) if own else dst
        return remote(src, dst, c_send.at[u, zs, xs], c_recv.at[u, zs, xs], c_peer)

    def spread(u, zs, own=False):
        x_copy(u, zs, own).start()

        c_copy(u, zs, col, own).start()

    def own_sends(u):
        @pl.when(can_up[u])
        def _():
            z_copy(u, z, 0, True).start()

        @pl.when(can_down[u])
        def _():
            z_copy(u, z, 1, True).start()

        if u != 4:
            spread(u, z, True)

    def z_events(u):
        for step in range(1, nz):
            @pl.when((z - step >= 0) if u != 4 else (z - step >= 0) & (low == 0))
            def _():
                zs = z - step
                z_copy(u, zs, 0).wait_recv()

                @pl.when(can_up[u])
                def _():
                    z_copy(u, zs, 0).start()

                if u != 4:
                    spread(u, zs)

            @pl.when((z + step < nz) if u != 4 else (z + step < nz) & (low == 1))
            def _():
                zs = z + step
                z_copy(u, zs, 1).wait_recv()

                @pl.when(can_down[u])
                def _():
                    z_copy(u, zs, 1).start()

                if u != 4:
                    spread(u, zs)

    def x_events(u):
        for step in range(nz):
            zs = 2 * ((z // 2 + step // 2) % (nz // 2)) + (z % 2 + step % 2) % 2
            dst = place(u, zs, 1 - col, core)

            remote(dst, dst, x_send.at[u, zs], x_recv.at[u, zs], x_peer).wait_recv()
            c_copy(u, zs, 1 - col).start()

    def c_waits(u):
        for xs in range(2):
            for zs in range(nz):
                dst = place(u, zs, xs, 1 - core)
                remote(dst, dst, c_send.at[u, zs, xs], c_recv.at[u, zs, xs], c_peer).wait_recv()

    fill = [
        pltpu.make_async_copy(head_ref, head_own.at[:, pl.ds(0, width)], own_sem.at[0]),
        pltpu.make_async_copy(bias_ref, head_own.at[:, pl.ds(width, LANES)], own_sem.at[1]),
    ]
    for copy in fill:
        copy.start()
    barrier = pltpu.get_barrier_semaphore()
    for off in range(1, n):
        pl.semaphore_signal(barrier, inc=1, device_id={"seq": (me + off) % n}, device_id_type=MESH)
    pl.semaphore_signal(barrier, inc=1, device_id={"grp": 1 - grp}, device_id_type=MESH)
    pl.semaphore_wait(barrier, n)

    own_sends(0)
    own_sends(4)
    own_sends(1)
    for copy in fill:
        copy.wait()
    rows_of = [pl.ds(pl.multiple_of(me * depths[u], depths[u]), depths[u]) for u in range(4)]
    convf[tap, rows_of[0], :] = conv_ref[tap]
    convf[1, rows_of[1], :] = conv_ref[1]
    projf[rows_of[2], :] = proj_ref[...]
    headf[rows_of[3], :] = head_own[...]
    xf = x_ref[...].astype(jnp.float32)
    scale = lax.rsqrt(jnp.mean(xf * xf, axis=-1, keepdims=True) + EPS)
    normed[...] = (xf * scale * gain_ref[...]).astype(jnp.bfloat16)
    z_events(4)
    z_events(0)
    own_sends(2)
    own_sends(3)
    z_events(1)
    z_events(2)
    z_events(3)
    x_events(0)
    c_waits(0)

    chunks = q_out.shape[0]
    wide = inner // chunks

    def q_copy(k):
        return remote(q_out.at[k], q_in.at[k], q_send.at[k], q_recv.at[k], partner)

    def g_copy(k):
        return remote(pg.at[k], pg_in.at[k], g_send.at[k], g_recv.at[k], partner)

    for k in range(chunks):
        cols = slice(k * wide, (k + 1) * wide)
        q_out[k] = dot_nn(normed[...], convf[tap, :, cols]).astype(jnp.bfloat16)
        q_copy(k).start()
    x_events(1)
    c_waits(1)
    for k in range(chunks):
        cols = slice(k * wide, (k + 1) * wide)
        pre[:, cols] = dot_nn(normed[...], convf[1, :, cols])
    x_events(2)
    x_events(3)
    for k in range(chunks):
        cols = slice(k * wide, (k + 1) * wide)
        q_copy(k).wait_recv()
        v = pre[:, cols] + q_in[k].astype(jnp.float32)
        pre[:, cols] = v
        act[:, cols] = (0.5 * v * (1.0 + jnp.tanh(GELU_K * (v + GELU_C * v * v * v)))).astype(jnp.bfloat16)
    c_waits(2)
    for k in range(width // 512):
        cols = slice(k * 512, (k + 1) * 512)
        stream[:, cols] = (
            x_ref[:, cols].astype(jnp.float32) + back_dot(act[...], projf[cols, :])
        ).astype(jnp.bfloat16)
    lane = lax.broadcasted_iota(jnp.int32, (rows, LANES), 1)
    stream[:, width:] = jnp.where(lane == 0, 1.0, 0.0).astype(jnp.bfloat16)
    c_waits(3)
    logits = back_dot(stream[...], headf[...])
    expo = jnp.exp(-jnp.abs(logits))
    rate = jnp.maximum(logits, 0.0) + jnp.log1p(expo) + 0.05
    seen = counts_ref[...].astype(jnp.float32)
    terms = rate - seen * jnp.log(rate)
    losses[me] = jnp.broadcast_to(jnp.sum(terms), losses.shape[1:])
    inv = 1.0 / (1.0 + expo)
    sig = jnp.where(logits >= 0, inv, expo * inv)
    lg = ((1.0 - seen / rate) * sig).astype(jnp.bfloat16)

    def l_copy(off):
        return remote(losses.at[me], losses.at[me], l_send.at[off], l_recv.at[me], (me + off) % n)

    for off in range(1, n):
        l_copy(off).start()
    for k in range(width // 512):
        cols = slice(k * 512, (k + 1) * 512)
        part = dot_nn(lg, headf[:, cols])
        res[:, cols] = part
        normed[:, cols] = part.astype(jnp.bfloat16)
    for k in range(chunks):
        cols = slice(k * wide, (k + 1) * wide)
        ag = dot_nn(normed[...], projf[:, cols])
        v = pre[:, cols]
        th = jnp.tanh(GELU_K * (v + GELU_C * v * v * v))
        slope = 0.5 * (1.0 + th) + 0.5 * v * (1.0 - th * th) * (GELU_K * (1.0 + 3.0 * GELU_C * v * v))
        pg[k] = (ag * slope).astype(jnp.bfloat16)
        g_copy(k).start()
    for k in range(width // 512):
        cols = slice(k * 512, (k + 1) * 512)
        total = back_dot(pg[0], convf[1, cols, :wide])
        for j in range(1, chunks):
            total = total + back_dot(pg[j], convf[1, cols, j * wide:(j + 1) * wide])
        ng[:, cols] = total
    for j in range(chunks):
        g_copy(j).wait_recv()
        for k in range(width // 512):
            cols = slice(k * 512, (k + 1) * 512)
            ng[:, cols] += back_dot(pg_in[j], convf[tap, cols, j * wide:(j + 1) * wide])
    xf = x_ref[...].astype(jnp.float32)
    scale = lax.rsqrt(jnp.mean(xf * xf, axis=-1, keepdims=True) + EPS)
    dy = ng[...] * gain_ref[...]
    inner_mean = jnp.mean(xf * dy, axis=-1, keepdims=True)
    out_ref[...] = (res[...] + (scale * dy - xf * (scale * scale * scale * inner_mean))).astype(jnp.bfloat16)

    for off in range(1, n):
        source = (me + off) % n
        remote(losses.at[source], losses.at[source], l_send.at[off], l_recv.at[source], source).wait_recv()
    total = losses[0]
    for k in range(1, n):
        total = total + losses[k]
    loss_ref[0] = total[0, 0] * (1.0 / bins_total)

    for off in range(1, n):
        l_copy(off).wait_send()
    for k in range(chunks):
        q_copy(k).wait_send()
        g_copy(k).wait_send()
    for u in range(5):
        for zs in range(nz):
            @pl.when(can_up[u] & (zs <= z))
            def _():
                z_copy(u, zs, 0).wait_send()

            @pl.when(can_down[u] & (zs >= z))
            def _():
                z_copy(u, zs, 1).wait_send()

            if u != 4:
                x_copy(u, zs).wait_send()

                for xs in range(2):
                    c_copy(u, zs, xs).wait_send()


def paired(inputs, gain, conv_weight, proj_weight, head_weight, track_head_bias, counts):
    n = lax.axis_size("seq")
    seq_count, row_count, width = inputs.shape
    rows = seq_count * row_count
    tracks = counts.shape[2]
    inner = conv_weight.shape[2]
    nz = n // 4
    chunks = 3 if inner % (3 * LANES) == 0 else 1
    bias_t = jnp.pad(track_head_bias.T, ((0, 0), (0, LANES - 1)))
    vmem = pl.BlockSpec(memory_space=pltpu.VMEM)
    bf, f32 = jnp.bfloat16, jnp.float32
    dma = pltpu.SemaphoreType.DMA
    out, loss = pl.pallas_call(
        functools.partial(block_kernel, n, rows * n * tracks),
        out_shape=(
            jax.ShapeDtypeStruct((rows, width), bf),
            jax.ShapeDtypeStruct((1,), f32),
        ),
        in_specs=[vmem] * 7,
        out_specs=(vmem, pl.BlockSpec(memory_space=pltpu.SMEM)),
        scratch_shapes=[
            pltpu.VMEM((3, conv_weight.shape[1] * n, inner), bf),
            pltpu.VMEM((width, inner), bf),
            pltpu.VMEM((tracks, width + LANES), bf),
            pltpu.VMEM((tracks // n, width + LANES), bf),
            pltpu.VMEM((rows, width), bf),
            pltpu.VMEM((chunks, rows, inner // chunks), bf),
            pltpu.VMEM((chunks, rows, inner // chunks), bf),
            pltpu.VMEM((rows, inner), f32),
            pltpu.VMEM((rows, inner), bf),
            pltpu.VMEM((rows, width + LANES), bf),
            pltpu.VMEM((rows, width), f32),
            pltpu.VMEM((chunks, rows, inner // chunks), bf),
            pltpu.VMEM((chunks, rows, inner // chunks), bf),
            pltpu.VMEM((rows, width), f32),
            pltpu.VMEM((n, 8, LANES), f32),
            dma((5, nz, 2)), dma((5, nz)), dma((4, nz)), dma((4, nz)),
            dma((4, nz)), dma((4, nz)), dma((4, nz, 2)), dma((4, nz, 2)),
            dma((chunks,)), dma((chunks,)), dma((chunks,)), dma((chunks,)),
            dma((n,)), dma((n,)), dma((2,)),
        ],
        compiler_params=pltpu.CompilerParams(
            collective_id=0, has_side_effects=True, vmem_limit_bytes=58 * 1024 * 1024
        ),
    )(
        inputs.reshape(rows, width), gain.reshape(1, width), conv_weight, proj_weight.T,
        head_weight.T, bias_t, counts.reshape(rows, tracks),
    )
    return out.reshape(inputs.shape), loss


def fits(mesh, conv_weight, proj_weight, head_weight, inputs):
    n = mesh.shape["seq"]
    shard = conv_weight.shape[1] // n
    return (
        n == 2 * SPAN
        and mesh.shape["grp"] == 2
        and shard % 16 == 0
        and (head_weight.shape[1] // n) % 16 == 0
        and inputs.shape[2] % 512 == 0
        and head_weight.shape[1] <= 1024
    )


def solution(mesh):
    placed = (
        P("grp", "seq", None),
        P(),
        P(None, "seq", None),
        P(None, "seq"),
        P(None, "seq"),
        P(None, "seq"),
        P("grp", "seq", None),
    )

    def run(inputs, gain, conv_weight, proj_weight, head_weight, track_head_bias, counts):
        whole = fits(mesh, conv_weight, proj_weight, head_weight, inputs)
        return jax.shard_map(
            paired if whole else shards,
            mesh=mesh,
            in_specs=placed,
            out_specs=(P("grp", "seq", None), P("grp")),
            check_vma=False,
        )(inputs, gain, conv_weight, proj_weight, head_weight, track_head_bias, counts)

    return run
```
